256 devices in a mesh: row: 32 (over x, z_lo, y), col: 8 (over z_hi, core).
Axes of the slice: x: 4, y: 4, z: 8 (z_hi: 4, z_lo: 2; z = z_hi * 2 + z_lo), core: 2. Of those that a mesh axis runs over, the one named last changes fastest.
Arguments:
- root_cov: float32 [6144, 6144], P('row', 'col'), as said below
- structure: int32 [16], replicated, may hold values from 0 to 47, as said below
- child_factor: float32 [2048, 4096], P('row', 'col'), may hold values from -0.9 to 0.9
- child_diag: float32 [4096, 4096], P('row', 'col'), may hold values from -6 to 6
Outputs:
- cross_cov: float32 [2048, 4096], P('row', 'col')
- child_cov: float32 [4096, 4096], P('row', 'col')
The draws below stay inside these ranges and needn't reach their ends.
Inputs may be any that keep to these rules, and one draw needn't show every extreme that they name: root_cov is exactly symmetric and positive definite; its off-diagonal entries are small against its diagonal, which is about 1.5 times the product of a row scale and a column scale. `structure`: 16 distinct tiles in increasing order; the first and the last tile of the root are always among them, and so is tile R // 256 + 2 * R // 2048, which is the third tile of the list.
All inputs are finite; a program needn't handle non-finite values.
Results may differ from the reference program's by a relative error of at most 0.000078.
Values sent between devices are 32-bit elements; how exact they have to be, the bound alone decides.
No kernel may reach another device: no remote copies, remote signals or barrier semaphores. Data moves between devices by JAX's collectives and lax.ppermute only.
A program may use at most 64 MiB of HBM per device.

```python
import math
import jax
import jax.numpy as jnp
from jax import lax

R = 6144
C = 4096
BLK = 128
KB = 16
K = 2048


def draw_root_cov(key, part):
    key_base = jax.random.fold_in(key, 11)
    base_draw = jax.random.normal(key_base, (R, R), jnp.float32)
    symmetric = (base_draw + base_draw.T) * (0.5 / math.sqrt(R))
    diagonal_mask = lax.iota(jnp.int32, R)[:, None] == lax.iota(jnp.int32, R)[None, :]
    core_matrix = jnp.where(diagonal_mask, 1.5, symmetric)
    return core_matrix.astype(jnp.float32)


def draw_structure(key, part):
    tile_count = R // BLK
    key_tile = tile_count // 2 + 2 * tile_count // KB
    lower_tile = jax.random.randint(jax.random.fold_in(key, 21), (1,), 1, key_tile).astype(jnp.int32)
    upper_pool = jax.random.permutation(jax.random.fold_in(key, 22), tile_count - key_tile - 2) + key_tile + 1
    upper_tiles = jnp.sort(upper_pool[:KB - 4]).astype(jnp.int32)
    first_tile = jnp.zeros((1,), jnp.int32)
    middle_tile = jnp.full((1,), key_tile, jnp.int32)
    last_tile = jnp.full((1,), tile_count - 1, jnp.int32)
    return jnp.concatenate([first_tile, lower_tile, middle_tile, upper_tiles, last_tile]).astype(jnp.int32)


def block_scale(own_key, dims, cuts, least, top_value):
    loudness, own = 1.0, jax.random.fold_in(own_key, 6)
    for axis_at, blocks in cuts:
        steps = jnp.exp(jax.random.uniform(jax.random.fold_in(own, axis_at), (blocks,), jnp.float32, least / len(cuts), top_value / len(cuts)))
        loudness = loudness * jnp.repeat(steps, dims[axis_at] // blocks).reshape([-1 if axis == axis_at else 1 for axis in range(len(dims))])
    return loudness


def gaussian(key, extent, scale, most, shards=(), kind=jnp.bfloat16):
    array = jax.random.normal(key, extent, jnp.float32) * scale
    if len(shards) > 0:
        array = block_scale(key, extent, shards, -0.22, 0.18) * array
    return jnp.clip(array, min=-most, max=most).astype(kind)


def setup_inputs(seed: int = 0) -> dict:
    key_list = jax.random.split(jax.random.key(seed), 5)
    root_cov = draw_root_cov(jax.random.fold_in(key_list[4], 71), 0)
    structure = draw_structure(jax.random.fold_in(key_list[4], 71), 0)
    child_factor = gaussian(key_list[2], (K, C), 0.15, 0.9, ((0, 32), (1, 8)), jnp.float32)
    child_diag = gaussian(key_list[3], (C, C), 1.0, 6.0, ((0, 32), (1, 8)), jnp.float32)
    return {"root_cov": root_cov, "structure": structure, "child_factor": child_factor, "child_diag": child_diag}


def reference(root_cov, structure, child_factor, child_diag):
    offsets = jnp.arange(BLK, dtype=jnp.int32)
    struct_rows = (structure[:, None] * BLK + offsets[None, :]).reshape(-1).astype(jnp.int32)
    selected = jnp.take(jnp.take(root_cov, struct_rows, axis=0), struct_rows, axis=1)
    cross_cov = -jnp.dot(selected, child_factor, precision=lax.Precision.HIGHEST, preferred_element_type=jnp.float32)
    product = jnp.dot(child_factor.T, cross_cov, precision=lax.Precision.HIGHEST, preferred_element_type=jnp.float32)
    child_cov = child_diag - product
    return (cross_cov, child_cov)
```

```python
import jax
import jax.numpy as jnp
from jax import lax
from jax.experimental import pallas as pl
from jax.experimental.pallas import tpu as pltpu
from jax.sharding import Mesh, PartitionSpec as P

BLK = 128
AXES = ("x", "zl", "y", "zh", "core")
SIZES = (4, 2, 4, 4, 2)
ROWS = ("x", "zl", "y")
COLS = ("zh", "core")
GROUP = ("x", "zl")
HI = lax.Precision.HIGHEST


def spread_kernel(table, wide, out):
    for p in range(16):
        owner = table[p]
        column = pl.multiple_of(table[16 + p], BLK)
        for y in range(4):
            row = pl.multiple_of(table[32 + y], 8)
            out[(p // 2) * 4 + y, :, (p % 2) * BLK:(p % 2 + 1) * BLK] = wide[
                owner, pl.ds(row, 8), pl.ds(column, BLK)
            ]


def pick_kernel(table, pieces, out):
    for j in range(8):
        out[j] = pieces[table[j]]


def contract(first, second):
    return lax.dot_general(
        first, second, (((0,), (0,)), ((), ())), precision=HI, preferred_element_type=jnp.float32
    )


def vmem():
    return pl.BlockSpec(memory_space=pltpu.VMEM)


def smem():
    return pl.BlockSpec(memory_space=pltpu.SMEM)


def gather_group(block):
    copies = jnp.broadcast_to(block[None], (8,) + block.shape)
    return lax.all_to_all(copies, GROUP, 0, 0).reshape(-1, block.shape[1])


def per_device(root_cov, structure, child_factor, child_diag):
    y = lax.axis_index("y")
    row_dev = (lax.axis_index("x") * 2 + lax.axis_index("zl")) * 4 + y

    factor_mine = lax.all_gather(child_factor, GROUP, axis=0, tiled=True)
    turn = []
    for a in range(8):
        for b in range(4):
            for c in range(8):
                turn.append(((a * 4 + b) * 8 + c, (c * 4 + b) * 8 + a))
    turned = lax.ppermute(child_factor, AXES, turn)

    halves = row_dev * 3 + lax.iota(jnp.int32, 3)
    tiles = halves // 2
    position = jnp.sum((structure[None, :] < tiles[:, None]).astype(jnp.int32), axis=1)
    member = jnp.any(structure[None, :] == tiles[:, None], axis=1)
    kind = jnp.where(member, (2 * position + halves % 2) % 4, -1)
    classes = lax.iota(jnp.int32, 4)
    slot = jnp.sum(
        jnp.where(kind[None, :] == classes[:, None], lax.iota(jnp.int32, 3)[None, :], 0), axis=1
    )
    table = jnp.concatenate([structure // 6, structure % 6 * BLK, slot * 8])

    shares = root_cov.reshape(3, 8, 8, 768).transpose(1, 0, 2, 3).reshape(8, 24, 768)
    wide = lax.all_to_all(shares, COLS, 0, 0)
    wide, turned = lax.optimization_barrier((wide, turned))
    factor_turned = lax.all_gather(turned, COLS, axis=0, tiled=True)
    sends = pl.pallas_call(
        spread_kernel,
        out_shape=jax.ShapeDtypeStruct((32, 8, 256), jnp.float32),
        in_specs=[smem(), vmem()],
        out_specs=vmem(),
    )(table, wide)
    pieces = lax.all_to_all(sends, ROWS, 0, 0)
    steps = 2 * lax.iota(jnp.int32, 8) + y // 2
    sources = (2 * jnp.take(structure, steps) + y % 2) // 3
    piece = pl.pallas_call(
        pick_kernel,
        out_shape=jax.ShapeDtypeStruct((8, 8, 256), jnp.float32),
        in_specs=[smem(), vmem()],
        out_specs=vmem(),
    )(sources, pieces)
    parts = [piece]
    zh = lax.axis_index("zh")
    for k in range(1, 4):
        parts.append(lax.ppermute(piece, "zh", [(i, (i + k) % 4) for i in range(4)]))
    near = jnp.stack(parts)
    far = lax.ppermute(near, "core", [(0, 1), (1, 0)])
    core = lax.axis_index("core")
    first = jnp.where(core == 0, near, far)
    second = jnp.where(core == 0, far, near)
    both = jnp.stack([first, second], axis=1)
    order = (zh - lax.iota(jnp.int32, 4)) % 4
    both = jnp.take(both, order, axis=0)
    brick = both.reshape(8, 8, 8, 256).transpose(1, 0, 2, 3).reshape(512, 256)

    share = contract(brick, factor_mine)
    got = lax.all_to_all(share.reshape(4, 64, 512), "y", 0, 0)
    cross = -(got[0] + got[1] + got[2] + got[3])
    cross_group = gather_group(cross)
    share = contract(factor_turned, cross_group)
    got = lax.all_to_all(share.reshape(4, 128, 512), "y", 0, 0)
    child = child_diag - (got[0] + got[1] + got[2] + got[3])
    return cross, child


def solution(mesh):
    fine = Mesh(mesh.devices.reshape(SIZES), AXES)
    spec = P(ROWS, COLS)
    return jax.shard_map(
        per_device,
        mesh=fine,
        in_specs=(spec, P(), spec, spec),
        out_specs=(spec, spec),
        check_vma=False,
    )
```

```python
import jax
import jax.numpy as jnp
from jax import lax
from jax.experimental import pallas as pl
from jax.experimental.pallas import tpu as pltpu
from jax.sharding import Mesh, PartitionSpec as P

BLK = 128
AXES = ("x", "zl", "y", "zh", "core")
SIZES = (4, 2, 4, 4, 2)
ROWS = ("x", "zl", "y")
COLS = ("zh", "core")
GROUP = ("x", "zl")
SWAP = [(0, 1), (1, 0)]
HI = lax.Precision.HIGHEST


def spread_kernel(table, keep, got, out):
    for p in range(16):
        source = table[p]
        column = pl.multiple_of(table[16 + p], BLK)
        own = table[32 + p] == 1
        for y in range(4):
            slot = table[48 + y]
            here = keep[source, slot, :, pl.ds(column, BLK)]
            there = got[source, slot, :, pl.ds(column, BLK)]
            out[(p // 2) * 4 + y, :, (p % 2) * BLK:(p % 2 + 1) * BLK] = jnp.where(own, here, there)


def pick_kernel(table, pieces, out):
    for j in range(8):
        out[j] = pieces[table[j]]


def contract(first, second):
    return lax.dot_general(
        first, second, (((0,), (0,)), ((), ())), precision=HI, preferred_element_type=jnp.float32
    )


def vmem():
    return pl.BlockSpec(memory_space=pltpu.VMEM)


def smem():
    return pl.BlockSpec(memory_space=pltpu.SMEM)


def shift(block, axis, k):
    return lax.ppermute(block, axis, [(i, (i + k) % 4) for i in range(4)])


def in_order(slots, index):
    return jnp.take(slots, (index - lax.iota(jnp.int32, 4)) % 4, axis=0)


def gather_cols_finish(parts, zh, core):
    near = jnp.stack(parts)
    far = lax.ppermute(near, "core", SWAP)
    first = jnp.where(core == 0, near, far)
    second = jnp.where(core == 0, far, near)
    both = in_order(jnp.stack([first, second], axis=1), zh)
    return both.reshape((8,) + both.shape[2:])


def per_device(root_cov, structure, child_factor, child_diag):
    x, zl, y = lax.axis_index("x"), lax.axis_index("zl"), lax.axis_index("y")
    zh, core = lax.axis_index("zh"), lax.axis_index("core")
    row_dev = (x * 2 + zl) * 4 + y

    halves = row_dev * 3 + lax.iota(jnp.int32, 3)
    tiles = halves // 2
    position = jnp.sum((structure[None, :] < tiles[:, None]).astype(jnp.int32), axis=1)
    member = jnp.any(structure[None, :] == tiles[:, None], axis=1)
    kind = jnp.where(member, (2 * position + halves % 2) % 4, -1)
    classes = lax.iota(jnp.int32, 4)
    slot = jnp.sum(
        jnp.where(kind[None, :] == classes[:, None], lax.iota(jnp.int32, 3)[None, :], 0), axis=1
    )
    owner = structure // 6
    table = jnp.concatenate([
        (zh - owner // 2) % 4,
        structure % 6 * BLK,
        (owner % 2 == core).astype(jnp.int32),
        slot,
    ])
    steps = 2 * lax.iota(jnp.int32, 8) + y // 2
    sources = (2 * jnp.take(structure, steps) + y % 2) // 3

    shares = root_cov.reshape(3, 4, 16, 768)
    mine = [lax.dynamic_index_in_dim(shares, (zh + k) % 4, 1, keepdims=False) for k in range(4)]
    landed = [mine[0]] + [shift(mine[k], "zh", k) for k in (1, 2, 3)]
    factor_pair = lax.ppermute(child_factor, "zl", SWAP)
    landed = jnp.stack(landed).reshape(4, 3, 2, 8, 768)
    keep = lax.dynamic_index_in_dim(landed, core, 2, keepdims=False)
    give = lax.dynamic_index_in_dim(landed, 1 - core, 2, keepdims=False)
    got = lax.ppermute(give, "core", SWAP)
    sends = pl.pallas_call(
        spread_kernel,
        out_shape=jax.ShapeDtypeStruct((32, 8, 256), jnp.float32),
        in_specs=[smem(), vmem(), vmem()],
        out_specs=vmem(),
    )(table, keep, got)

    sends, factor_pair, factor = lax.optimization_barrier((sends, factor_pair, child_factor))
    pieces = lax.all_to_all(sends, ROWS, 0, 0)
    pair = jnp.stack(
        [jnp.where(zl == 0, factor, factor_pair), jnp.where(zl == 0, factor_pair, factor)]
    )
    factor_x = [pair] + [shift(pair, "x", k) for k in (1, 2, 3)]
    turn = []
    for a in range(8):
        for b in range(4):
            for c in range(8):
                turn.append(((a * 4 + b) * 8 + c, (c * 4 + b) * 8 + a))
    turned = lax.ppermute(factor, AXES, turn)
    pieces, factor_x, turned = lax.optimization_barrier((pieces, factor_x, turned))

    piece = pl.pallas_call(
        pick_kernel,
        out_shape=jax.ShapeDtypeStruct((8, 8, 256), jnp.float32),
        in_specs=[smem(), vmem()],
        out_specs=vmem(),
    )(sources, pieces)
    brick = gather_cols_finish([piece] + [shift(piece, "zh", k) for k in (1, 2, 3)], zh, core)
    brick = brick.transpose(1, 0, 2, 3).reshape(512, 256)
    factor_mine = in_order(jnp.stack(factor_x), x).reshape(512, 512)

    share = contract(brick, factor_mine)
    share, turned = lax.optimization_barrier((share, turned))
    got = lax.all_to_all(share.reshape(4, 64, 512), "y", 0, 0)
    turned_parts = [turned] + [shift(turned, "zh", k) for k in (1, 2, 3)]
    got, turned_parts = lax.optimization_barrier((got, turned_parts))
    cross = -(got[0] + got[1] + got[2] + got[3])
    copies = jnp.broadcast_to(cross[None], (8, 64, 512))
    cross_group = lax.all_to_all(copies, GROUP, 0, 0).reshape(512, 512)
    factor_turned = gather_cols_finish(turned_parts, zh, core).reshape(512, 512)
    share = contract(factor_turned, cross_group)
    got = lax.all_to_all(share.reshape(4, 128, 512), "y", 0, 0)
    child = child_diag - (got[0] + got[1] + got[2] + got[3])
    return cross, child


def solution(mesh):
    fine = Mesh(mesh.devices.reshape(SIZES), AXES)
    spec = P(ROWS, COLS)
    return jax.shard_map(
        per_device,
        mesh=fine,
        in_specs=(spec, P(), spec, spec),
        out_specs=(spec, spec),
        check_vma=False,
    )
```

```python
import jax
import jax.numpy as jnp
from jax import lax
from jax.experimental import pallas as pl
from jax.experimental.pallas import tpu as pltpu
from jax.sharding import Mesh, PartitionSpec as P

BLK = 128
AXES = ("x", "zl", "y", "zh", "core")
SIZES = (4, 2, 4, 4, 2)
CLASSED = ("y", "x", "zl")
ROWS = ("x", "zl", "y")
COLS = ("zh", "core")
GROUP = ("x", "zl")
SWAP = [(0, 1), (1, 0)]
HI = lax.Precision.HIGHEST


def class_kernel(where, structure, root, out, sems):
    row_dev = where[0]
    place = []
    for k in range(3):
        half = row_dev * 3 + k
        tile = half // 2
        before = jnp.int32(0)
        member = jnp.int32(0)
        for i in range(16):
            before += (structure[i] < tile).astype(jnp.int32)
            member += (structure[i] == tile).astype(jnp.int32)
        place.append(jnp.where(member > 0, (2 * before + half % 2) % 4, -1))
    copies = []
    for y in range(4):
        k = jnp.where(place[1] == y, 1, jnp.where(place[2] == y, 2, 0))
        copies.append(
            pltpu.make_async_copy(root.at[pl.ds(pl.multiple_of(k * 64, 64), 64)], out.at[y], sems.at[y])
        )
    for copy in copies:
        copy.start()
    for copy in copies:
        copy.wait()


def cut_kernel(table, pieces, own, down, down_two):
    zh = table[24]
    for d, out in enumerate((own, down, down_two)):
        for q in range(4):
            place = 4 * jnp.maximum(zh - d, 0) + q
            column = pl.multiple_of(table[8 + place], BLK)
            for j in range(8):
                out[q // 2, j, :, (q % 2) * BLK:(q % 2 + 1) * BLK] = pieces[table[j], :, pl.ds(column, BLK)]


def contract(first, second):
    return lax.dot_general(
        first, second, (((0,), (0,)), ((), ())), precision=HI, preferred_element_type=jnp.float32
    )


def vmem():
    return pl.BlockSpec(memory_space=pltpu.VMEM)


def smem():
    return pl.BlockSpec(memory_space=pltpu.SMEM)


def anywhere():
    return pl.BlockSpec(memory_space=pl.ANY)


def shift(block, axis, k):
    return lax.ppermute(block, axis, [(i, (i + k) % 4) for i in range(4)])


def turn(block, k):
    pairs = []
    for a in range(8):
        for b in range(4):
            for c in range(8):
                target = (a // 2 - k) % 4 * 2 + a % 2
                pairs.append(((a * 4 + b) * 8 + c, (c * 4 + b) * 8 + target))
    return lax.ppermute(block, AXES, pairs)


def at(array, index, axis=0):
    return lax.dynamic_index_in_dim(array, index, axis, keepdims=False)


def per_device(root_cov, structure, child_factor, child_diag):
    x, zl, y = lax.axis_index("x"), lax.axis_index("zl"), lax.axis_index("y")
    zh, core = lax.axis_index("zh"), lax.axis_index("core")
    group, col = x * 2 + zl, zh * 2 + core
    fours = lax.iota(jnp.int32, 4)

    turned = [turn(child_factor, k) for k in range(4)]

    sends = pl.pallas_call(
        class_kernel,
        out_shape=jax.ShapeDtypeStruct((4, 64, 768), jnp.float32),
        in_specs=[smem(), smem(), anywhere()],
        out_specs=anywhere(),
        scratch_shapes=[pltpu.SemaphoreType.DMA((4,))],
    )((group * 4 + y)[None], structure, root_cov)
    pieces = lax.all_to_all(sends.reshape(32, 8, 768), CLASSED, 0, 0)
    pieces, turned = lax.optimization_barrier((pieces, turned))

    steps = 2 * lax.iota(jnp.int32, 8) + y // 2
    source = (2 * jnp.take(structure, steps) + y % 2) // 3
    table = jnp.concatenate([source % 4 * 8 + source // 4, structure % 6 * BLK, zh[None]])
    cut = jax.ShapeDtypeStruct((2, 8, 8, 256), jnp.float32)
    own, down, down_two = pl.pallas_call(
        cut_kernel,
        out_shape=(cut, cut, cut),
        in_specs=[smem(), vmem()],
        out_specs=(vmem(), vmem(), vmem()),
    )(table, pieces)
    down = lax.ppermute(down, COLS, [(7, 5), (6, 4), (5, 3), (3, 1), (2, 0)])
    down_two = lax.ppermute(down_two, COLS, [(6, 2), (5, 1), (4, 0)])
    near = jnp.stack(turned)
    far = lax.ppermute(near, "core", SWAP)
    factor_x = [child_factor] + [shift(child_factor, "x", k) for k in (1, 2, 3)]
    down, down_two, near, far, factor_x = lax.optimization_barrier(
        (down, down_two, near, far, factor_x)
    )
    holder = structure // 6
    hops = lax.dynamic_slice(holder // 2, (4 * zh,), (4,)) - zh
    hops = jnp.repeat(hops, BLK).reshape(2, 1, 1, 256)
    mine = jnp.where(hops == 0, own, jnp.where(hops == 1, down, down_two))
    keep, give = at(mine, core), at(mine, 1 - core)
    got = lax.ppermute(give, "core", SWAP)
    side = jnp.repeat(lax.dynamic_slice(holder % 2, (2 * col,), (2,)), BLK)
    piece = jnp.where(side == core, keep, got)

    brick = lax.all_to_all(jnp.broadcast_to(piece[None], (8, 8, 8, 256)), GROUP, 0, 0)
    both = jnp.stack([jnp.where(core == 0, near, far), jnp.where(core == 0, far, near)], axis=1)
    factor_turned = jnp.take(both, (fours - zh) % 4, axis=0)
    factor_turned = factor_turned.reshape(8, 8, 8, 512).transpose(1, 0, 2, 3).reshape(512, 512)
    brick, factor_turned = lax.optimization_barrier((brick, factor_turned))

    share = contract(brick.reshape(512, 256), factor_turned)
    row = jnp.stack(factor_x)
    share, row = lax.optimization_barrier((share, row))
    got = lax.all_to_all(share.reshape(4, 64, 512), "y", 0, 0)
    other = lax.ppermute(row, "zl", SWAP)
    got, other = lax.optimization_barrier((got, other))
    cross = -(got[0] + got[1] + got[2] + got[3])

    near = jnp.stack([cross] + [shift(cross, "zh", k) for k in (1, 2, 3)])
    far = lax.ppermute(near, "core", SWAP)
    order = (x - zh + fours) % 4
    same = jnp.take(jnp.where(zl == core, row, other), order, axis=0)
    opposite = jnp.take(jnp.where(zl == core, other, row), order, axis=0)
    share = contract(near.reshape(256, 512), same.reshape(256, 512))
    share = share + contract(far.reshape(256, 512), opposite.reshape(256, 512))
    share, cross = lax.optimization_barrier((share, cross))
    got = lax.all_to_all(share.reshape(4, 128, 512), "y", 0, 0)
    child = child_diag - (got[0] + got[1] + got[2] + got[3])
    return turn(cross, 0), child


def solution(mesh):
    fine = Mesh(mesh.devices.reshape(SIZES), AXES)
    spec = P(ROWS, COLS)
    return jax.shard_map(
        per_device,
        mesh=fine,
        in_specs=(spec, P(), spec, spec),
        out_specs=(spec, spec),
        check_vma=False,
    )
```

```python
import jax
import jax.numpy as jnp
from jax import lax
from jax.experimental import pallas as pl
from jax.experimental.pallas import tpu as pltpu
from jax.sharding import Mesh, PartitionSpec as P

BLK = 128
AXES = ("x", "zl", "y", "zh", "core")
SIZES = (4, 2, 4, 4, 2)
CLASSED = ("y", "x", "zl")
ROWS = ("x", "zl", "y")
COLS = ("zh", "core")
GROUP = ("x", "zl")
SWAP = [(0, 1), (1, 0)]
HI = lax.Precision.HIGHEST


def class_kernel(structure, root, out):
    row_dev = (lax.axis_index("x") * 2 + lax.axis_index("zl")) * 4 + lax.axis_index("y")
    place = []
    for k in range(3):
        half = row_dev * 3 + k
        tile = half // 2
        before = jnp.int32(0)
        member = jnp.int32(0)
        for i in range(16):
            before += (structure[i] < tile).astype(jnp.int32)
            member += (structure[i] == tile).astype(jnp.int32)
        place.append(jnp.where(member > 0, (2 * before + half % 2) % 4, -1))
    for y in range(4):
        k = jnp.where(place[1] == y, 1, jnp.where(place[2] == y, 2, 0))
        out[y] = root[pl.ds(pl.multiple_of(k * 64, 64), 64), :]


def cut_kernel(structure, pieces, *outs):
    zh, y = lax.axis_index("zh"), lax.axis_index("y")
    for k, out in enumerate(outs):
        for core in range(2):
            half = 2 * structure[2 * ((zh + k) % 4 * 2 + core) + y // 2] + y % 2
            source = half // 3
            out[core] = pieces[source % 4 * 8 + source // 4]


def columns_kernel(structure, own, one, two, three, got, out):
    zh, core, y = lax.axis_index("zh"), lax.axis_index("core"), lax.axis_index("y")
    for side in range(2):
        for k in range(4):
            group = (zh + k) % 4 * 2 + (core if side == 0 else 1 - core)
            tiles = []
            for t in range(2):
                tile = structure[2 * group + t]
                holder = tile // 6
                hop = (zh - holder // 2 + 4) % 4
                column = pl.multiple_of(tile % 6 * BLK, BLK)
                there = got[hop, :, pl.ds(column, BLK)]
                here = [ref[core, :, pl.ds(column, BLK)] for ref in (own, one, two, three)]
                here = jnp.where(hop == 0, here[0], jnp.where(hop == 1, here[1], jnp.where(hop == 2, here[2], here[3])))
                tiles.append(jnp.where(holder % 2 == core, here, there))
            pair = jnp.concatenate(tiles, axis=1)
            pair = pltpu.roll(pair, (4 - y) % 4 * 64, 1)
            out[:, (side * 4 + k) * 256:(side * 4 + k + 1) * 256] = pair


def dot(first, second, axis):
    return lax.dot_general(
        first, second, (((axis,), (0,)), ((), ())), precision=HI, preferred_element_type=jnp.float32
    )


def vmem():
    return pl.BlockSpec(memory_space=pltpu.VMEM)


def smem():
    return pl.BlockSpec(memory_space=pltpu.SMEM)


def anywhere():
    return pl.BlockSpec(memory_space=pl.ANY)


def shift(block, axis, k):
    return lax.ppermute(block, axis, [(i, (i + k) % 4) for i in range(4)])


def turn(block, k):
    pairs = []
    for a in range(8):
        for b in range(4):
            for c in range(8):
                target = (a // 2 - k) % 4 * 2 + a % 2
                pairs.append(((a * 4 + b) * 8 + c, (c * 4 + b) * 8 + target))
    return lax.ppermute(block, AXES, pairs)


def at(array, index, axis=0):
    return lax.dynamic_index_in_dim(array, index, axis, keepdims=False)


def call(kernel, shapes, structure, *operands):
    return pl.pallas_call(
        kernel,
        out_shape=shapes,
        in_specs=[smem()] + [vmem()] * len(operands),
        out_specs=jax.tree.map(lambda _: vmem(), shapes),
    )(structure, *operands)


def of(*shape):
    return jax.ShapeDtypeStruct(shape, jnp.float32)


def per_device(root_cov, structure, child_factor, child_diag):
    x, zl = lax.axis_index("x"), lax.axis_index("zl")
    zh, core = lax.axis_index("zh"), lax.axis_index("core")
    fours = lax.iota(jnp.int32, 4)

    sends = call(class_kernel, of(4, 64, 768), structure, root_cov)
    turned = [turn(child_factor, k) for k in range(4)]
    pieces = lax.all_to_all(sends.reshape(32, 8, 768), CLASSED, 0, 0)
    pieces, turned, factor = lax.optimization_barrier((pieces, turned, child_factor))

    cut = call(cut_kernel, [of(2, 8, 768)] * 4, structure, pieces)
    landed = [cut[0]] + [shift(cut[k], "zh", k) for k in (1, 2, 3)]
    give = jnp.stack([at(part, 1 - core) for part in landed])
    got = lax.ppermute(give, "core", SWAP)
    piece = call(columns_kernel, of(8, 2048), structure, *landed, got)
    other = lax.ppermute(factor, "zl", SWAP)

    rows = lax.all_to_all(jnp.broadcast_to(piece[None], (8, 8, 2048)), GROUP, 0, 0).reshape(64, 2048)

    turned = jnp.stack(turned)
    near = [turned] + [shift(turned, "y", -k) for k in (1, 2, 3)]
    far = [lax.ppermute(part, "core", SWAP) for part in near]
    near = jnp.stack(near, axis=1).reshape(1024, 512)
    far = jnp.stack(far, axis=1).reshape(1024, 512)

    cross = -(dot(rows[:, :1024], near, 1) + dot(rows[:, 1024:], far, 1))
    cross, factor, other = lax.optimization_barrier((cross, factor, other))

    near = jnp.stack([cross] + [shift(cross, "zh", -k) for k in (1, 2, 3)])
    far = lax.ppermute(near, "core", SWAP)
    pair = jnp.stack([jnp.where(zl == core, factor, other), jnp.where(zl == core, other, factor)])
    pairs = jnp.stack([pair] + [shift(pair, "x", -k) for k in (1, 2, 3)])
    pairs = jnp.take(pairs, (zh - x + fours) % 4, axis=0)
    share = dot(near.reshape(256, 512), pairs[:, 0].reshape(256, 512), 0)
    share = share + dot(far.reshape(256, 512), pairs[:, 1].reshape(256, 512), 0)
    share, cross = lax.optimization_barrier((share, cross))
    got = lax.all_to_all(share.reshape(4, 128, 512), "y", 0, 0)
    child = child_diag - (got[0] + got[1] + got[2] + got[3])
    return turn(cross, 0), child


def solution(mesh):
    fine = Mesh(mesh.devices.reshape(SIZES), AXES)
    spec = P(ROWS, COLS)
    return jax.shard_map(
        per_device,
        mesh=fine,
        in_specs=(spec, P(), spec, spec),
        out_specs=(spec, spec),
        check_vma=False,
    )
```

```python
import jax
import jax.numpy as jnp
from jax import lax
from jax.experimental import pallas as pl
from jax.experimental.pallas import tpu as pltpu
from jax.sharding import Mesh, PartitionSpec as P

BLK = 128
AXES = ("x", "zl", "y", "zh", "core")
SIZES = (4, 2, 4, 4, 2)
CLASSED = ("y", "x", "zl")
ROWS = ("x", "zl", "y")
COLS = ("zh", "core")
GROUP = ("x", "zl")
SWAP = [(0, 1), (1, 0)]
HI = lax.Precision.HIGHEST


def class_kernel(structure, root, out):
    row_dev = (lax.axis_index("x") * 2 + lax.axis_index("zl")) * 4 + lax.axis_index("y")
    place = []
    for k in range(3):
        half = row_dev * 3 + k
        tile = half // 2
        before = jnp.int32(0)
        member = jnp.int32(0)
        for i in range(16):
            before += (structure[i] < tile).astype(jnp.int32)
            member += (structure[i] == tile).astype(jnp.int32)
        place.append(jnp.where(member > 0, (2 * before + half % 2) % 4, -1))
    for y in range(4):
        k = jnp.where(place[1] == y, 1, jnp.where(place[2] == y, 2, 0))
        out[y] = root[pl.ds(pl.multiple_of(k * 64, 64), 64), :]


def cut_kernel(structure, pieces, *outs):
    zh, y = lax.axis_index("zh"), lax.axis_index("y")
    for k, out in enumerate(outs):
        for core in range(2):
            half = 2 * structure[2 * ((zh + k) % 4 * 2 + core) + y // 2] + y % 2
            source = half // 3
            out[core] = pieces[source % 4 * 8 + source // 4]


def columns_kernel(structure, own, one, two, three, got, out):
    zh, core, y = lax.axis_index("zh"), lax.axis_index("core"), lax.axis_index("y")
    for side in range(2):
        for k in range(4):
            group = (zh + k) % 4 * 2 + (core if side == 0 else 1 - core)
            tiles = []
            for t in range(2):
                tile = structure[2 * group + t]
                holder = tile // 6
                hop = (zh - holder // 2 + 4) % 4
                column = pl.multiple_of(tile % 6 * BLK, BLK)
                there = got[hop, :, pl.ds(column, BLK)]
                here = [ref[core, :, pl.ds(column, BLK)] for ref in (own, one, two, three)]
                here = jnp.where(hop == 0, here[0], jnp.where(hop == 1, here[1], jnp.where(hop == 2, here[2], here[3])))
                tiles.append(jnp.where(holder % 2 == core, here, there))
            pair = jnp.concatenate(tiles, axis=1)
            pair = pltpu.roll(pair, (4 - y) % 4 * 64, 1)
            out[:, (side * 4 + k) * 256:(side * 4 + k + 1) * 256] = pair


def dot(first, second, axis):
    return lax.dot_general(
        first, second, (((axis,), (0,)), ((), ())), precision=HI, preferred_element_type=jnp.float32
    )


def vmem():
    return pl.BlockSpec(memory_space=pltpu.VMEM)


def smem():
    return pl.BlockSpec(memory_space=pltpu.SMEM)


def anywhere():
    return pl.BlockSpec(memory_space=pl.ANY)


def shift(block, axis, k):
    return lax.ppermute(block, axis, [(i, (i + k) % 4) for i in range(4)])


def turn(block, k):
    pairs = []
    for a in range(8):
        for b in range(4):
            for c in range(8):
                target = (a // 2 - k) % 4 * 2 + a % 2
                pairs.append(((a * 4 + b) * 8 + c, (c * 4 + b) * 8 + target))
    return lax.ppermute(block, AXES, pairs)


def at(array, index, axis=0):
    return lax.dynamic_index_in_dim(array, index, axis, keepdims=False)


def call(kernel, shapes, structure, *operands):
    return pl.pallas_call(
        kernel,
        out_shape=shapes,
        in_specs=[smem()] + [vmem()] * len(operands),
        out_specs=jax.tree.map(lambda _: vmem(), shapes),
    )(structure, *operands)


def of(*shape):
    return jax.ShapeDtypeStruct(shape, jnp.float32)


def per_device(root_cov, structure, child_factor, child_diag):
    x, zl, y = lax.axis_index("x"), lax.axis_index("zl"), lax.axis_index("y")
    zh, core = lax.axis_index("zh"), lax.axis_index("core")

    sends = call(class_kernel, of(4, 64, 768), structure, root_cov)
    turned = [turn(child_factor, k) for k in range(4)]
    other = lax.ppermute(child_factor, "zl", SWAP)
    pieces = lax.all_to_all(sends.reshape(32, 8, 768), CLASSED, 0, 0)

    cut = call(cut_kernel, [of(2, 8, 768)] * 4, structure, pieces)
    landed = [cut[0]] + [shift(cut[k], "zh", k) for k in (1, 2, 3)]
    give = jnp.stack([at(part, 1 - core) for part in landed])
    got = lax.ppermute(give, "core", SWAP)
    piece = call(columns_kernel, of(8, 2048), structure, *landed, got)

    factor, other, turned, _ = lax.optimization_barrier((child_factor, other, jnp.stack(turned), cut))
    pair = jnp.stack([jnp.where(zl == core, factor, other), jnp.where(zl == core, other, factor)])
    block = jnp.stack([pair] + [shift(pair, "y", -k) for k in (1, 2, 3)], axis=1)
    columns = [block] + [shift(block, "x", -k) for k in (1, 2, 3)]

    near = [turned] + [shift(turned, "y", -k) for k in (1, 2, 3)]
    far = [lax.ppermute(part, "core", SWAP) for part in near]
    near = jnp.stack(near, axis=1).reshape(1024, 512)
    far = jnp.stack(far, axis=1).reshape(1024, 512)

    rows = lax.all_to_all(jnp.broadcast_to(piece[None], (8, 8, 2048)), GROUP, 0, 0).reshape(64, 2048)

    cross = -(dot(rows[:, :1024], near, 1) + dot(rows[:, 1024:], far, 1))

    slices = [lax.dynamic_slice(cross, (0, (y - k) % 4 * BLK), (64, BLK)) for k in range(4)]
    slab = jnp.stack([slices[0]] + [shift(slices[k], "y", -k) for k in (1, 2, 3)])
    near = jnp.stack([slab] + [shift(slab, "zh", -k) for k in (1, 2, 3)])
    far = lax.ppermute(near, "core", SWAP)
    cross, _ = lax.optimization_barrier((cross, slab))

    child = child_diag
    for side, held in enumerate((near, far)):
        for k in range(4):
            part = at(held, (x + k - zh) % 4).reshape(256, 128)
            child = child - dot(part, columns[k][side].reshape(256, 512), 0)
    return turn(cross, 0), child


def solution(mesh):
    fine = Mesh(mesh.devices.reshape(SIZES), AXES)
    spec = P(ROWS, COLS)
    return jax.shard_map(
        per_device,
        mesh=fine,
        in_specs=(spec, P(), spec, spec),
        out_specs=(spec, spec),
        check_vma=False,
    )
```

```python
import jax
import jax.numpy as jnp
from jax import lax
from jax.experimental import pallas as pl
from jax.experimental.pallas import tpu as pltpu
from jax.sharding import Mesh, PartitionSpec as P

BLK = 128
AXES = ("x", "zl", "y", "zh", "core")
SIZES = (4, 2, 4, 4, 2)
CLASSED = ("y", "x", "zl")
ROWS = ("x", "zl", "y")
COLS = ("zh", "core")
GROUP = ("x", "zl")
SWAP = [(0, 1), (1, 0)]
HI = lax.Precision.HIGH


def class_kernel(structure, root, out):
    row_dev = (lax.axis_index("x") * 2 + lax.axis_index("zl")) * 4 + lax.axis_index("y")
    place = []
    for k in range(3):
        half = row_dev * 3 + k
        tile = half // 2
        before = jnp.int32(0)
        member = jnp.int32(0)
        for i in range(16):
            before += (structure[i] < tile).astype(jnp.int32)
            member += (structure[i] == tile).astype(jnp.int32)
        place.append(jnp.where(member > 0, (2 * before + half % 2) % 4, -1))
    for y in range(4):
        k = jnp.where(place[1] == y, 1, jnp.where(place[2] == y, 2, 0))
        out[y] = root[pl.ds(pl.multiple_of(k * 64, 64), 64), :]


def cut_kernel(structure, pieces, *outs):
    zh, y = lax.axis_index("zh"), lax.axis_index("y")
    for k, out in enumerate(outs):
        for core in range(2):
            half = 2 * structure[2 * ((zh + k) % 4 * 2 + core) + y // 2] + y % 2
            source = half // 3
            out[core] = pieces[source % 4 * 8 + source // 4]


def columns_kernel(structure, own, one, two, three, got, out):
    zh, core, y = lax.axis_index("zh"), lax.axis_index("core"), lax.axis_index("y")
    for side in range(2):
        for k in range(4):
            group = (zh + k) % 4 * 2 + (core if side == 0 else 1 - core)
            tiles = []
            for t in range(2):
                tile = structure[2 * group + t]
                holder = tile // 6
                hop = (zh - holder // 2 + 4) % 4
                column = pl.multiple_of(tile % 6 * BLK, BLK)
                there = got[hop, :, pl.ds(column, BLK)]
                here = [ref[core, :, pl.ds(column, BLK)] for ref in (own, one, two, three)]
                here = jnp.where(hop == 0, here[0], jnp.where(hop == 1, here[1], jnp.where(hop == 2, here[2], here[3])))
                tiles.append(jnp.where(holder % 2 == core, here, there))
            pair = jnp.concatenate(tiles, axis=1)
            pair = pltpu.roll(pair, (4 - y) % 4 * 64, 1)
            out[:, (side * 4 + k) * 256:(side * 4 + k + 1) * 256] = pair


def dot(first, second, axis):
    return lax.dot_general(
        first, second, (((axis,), (0,)), ((), ())), precision=HI, preferred_element_type=jnp.float32
    )


def vmem():
    return pl.BlockSpec(memory_space=pltpu.VMEM)


def smem():
    return pl.BlockSpec(memory_space=pltpu.SMEM)


def anywhere():
    return pl.BlockSpec(memory_space=pl.ANY)


def shift(block, axis, k):
    return lax.ppermute(block, axis, [(i, (i + k) % 4) for i in range(4)])


def turn(block, k):
    pairs = []
    for a in range(8):
        for b in range(4):
            for c in range(8):
                target = (a // 2 - k) % 4 * 2 + a % 2
                pairs.append(((a * 4 + b) * 8 + c, (c * 4 + b) * 8 + target))
    return lax.ppermute(block, AXES, pairs)


def at(array, index, axis=0):
    return lax.dynamic_index_in_dim(array, index, axis, keepdims=False)


def call(kernel, shapes, structure, *operands):
    return pl.pallas_call(
        kernel,
        out_shape=shapes,
        in_specs=[smem()] + [vmem()] * len(operands),
        out_specs=jax.tree.map(lambda _: vmem(), shapes),
    )(structure, *operands)


def of(*shape):
    return jax.ShapeDtypeStruct(shape, jnp.float32)


def per_device(root_cov, structure, child_factor, child_diag):
    x, zl = lax.axis_index("x"), lax.axis_index("zl")
    zh, core = lax.axis_index("zh"), lax.axis_index("core")
    fours = lax.iota(jnp.int32, 4)

    sends = call(class_kernel, of(4, 64, 768), structure, root_cov)
    turned = [turn(child_factor, k) for k in range(4)]
    pieces = lax.all_to_all(sends.reshape(32, 8, 768), CLASSED, 0, 0)
    pieces, turned, factor = lax.optimization_barrier((pieces, turned, child_factor))

    cut = call(cut_kernel, [of(2, 8, 768)] * 4, structure, pieces)
    landed = [cut[0]] + [shift(cut[k], "zh", k) for k in (1, 2, 3)]
    give = jnp.stack([at(part, 1 - core) for part in landed])
    got = lax.ppermute(give, "core", SWAP)
    piece = call(columns_kernel, of(8, 2048), structure, *landed, got)
    other = lax.ppermute(factor, "zl", SWAP)

    rows = lax.all_to_all(jnp.broadcast_to(piece[None], (8, 8, 2048)), GROUP, 0, 0).reshape(64, 2048)

    turned = jnp.stack(turned)
    near = [turned] + [shift(turned, "y", -k) for k in (1, 2, 3)]
    far = [lax.ppermute(part, "core", SWAP) for part in near]
    near = jnp.stack(near, axis=1).reshape(1024, 512)
    far = jnp.stack(far, axis=1).reshape(1024, 512)

    cross = -(dot(rows[:, :1024], near, 1) + dot(rows[:, 1024:], far, 1))
    cross, factor, other = lax.optimization_barrier((cross, factor, other))

    near = jnp.stack([cross] + [shift(cross, "zh", -k) for k in (1, 2, 3)])
    far = lax.ppermute(near, "core", SWAP)
    pair = jnp.stack([jnp.where(zl == core, factor, other), jnp.where(zl == core, other, factor)])
    pairs = jnp.stack([pair] + [shift(pair, "x", -k) for k in (1, 2, 3)])
    pairs = jnp.take(pairs, (zh - x + fours) % 4, axis=0)
    share = dot(near.reshape(256, 512), pairs[:, 0].reshape(256, 512), 0)
    share = share + dot(far.reshape(256, 512), pairs[:, 1].reshape(256, 512), 0)
    share, cross = lax.optimization_barrier((share, cross))
    y = lax.axis_index("y")
    slabs = share.reshape(4, 128, 512)
    got = [at(slabs, y)] + [shift(at(slabs, (y + k) % 4), "y", k) for k in (1, 2, 3)]
    child = child_diag - (got[0] + got[1] + got[2] + got[3])
    return turn(cross, 0), child


def solution(mesh):
    fine = Mesh(mesh.devices.reshape(SIZES), AXES)
    spec = P(ROWS, COLS)
    return jax.shard_map(
        per_device,
        mesh=fine,
        in_specs=(spec, P(), spec, spec),
        out_specs=(spec, spec),
        check_vma=False,
    )
```

```python
import jax
import jax.numpy as jnp
from jax import lax
from jax.experimental import pallas as pl
from jax.experimental.pallas import tpu as pltpu
from jax.sharding import Mesh, PartitionSpec as P

BLK = 128
AXES = ("x", "zl", "y", "zh", "core")
SIZES = (4, 2, 4, 4, 2)
CLASSED = ("y", "x", "zl")
ROWS = ("x", "zl", "y")
COLS = ("zh", "core")
GROUP = ("x", "zl")
SWAP = [(0, 1), (1, 0)]
HI = lax.Precision.HIGH


def class_kernel(structure, root, out):
    row_dev = (lax.axis_index("x") * 2 + lax.axis_index("zl")) * 4 + lax.axis_index("y")
    place = []
    for k in range(3):
        half = row_dev * 3 + k
        tile = half // 2
        before = jnp.int32(0)
        member = jnp.int32(0)
        for i in range(16):
            before += (structure[i] < tile).astype(jnp.int32)
            member += (structure[i] == tile).astype(jnp.int32)
        place.append(jnp.where(member > 0, (2 * before + half % 2) % 4, -1))
    for y in range(4):
        k = jnp.where(place[1] == y, 1, jnp.where(place[2] == y, 2, 0))
        out[y] = root[pl.ds(pl.multiple_of(k * 64, 64), 64), :]


def cut_kernel(structure, pieces, *outs):
    zh, y = lax.axis_index("zh"), lax.axis_index("y")
    for k, out in enumerate(outs):
        for core in range(2):
            half = 2 * structure[2 * ((zh + k) % 4 * 2 + core) + y // 2] + y % 2
            source = half // 3
            out[core] = pieces[source % 4 * 8 + source // 4]


def columns_kernel(structure, own, one, two, three, got, out):
    zh, core, y = lax.axis_index("zh"), lax.axis_index("core"), lax.axis_index("y")
    for side in range(2):
        for k in range(4):
            group = (zh + k) % 4 * 2 + (core if side == 0 else 1 - core)
            tiles = []
            for t in range(2):
                tile = structure[2 * group + t]
                holder = tile // 6
                hop = (zh - holder // 2 + 4) % 4
                column = pl.multiple_of(tile % 6 * BLK, BLK)
                there = got[hop, :, pl.ds(column, BLK)]
                here = [ref[core, :, pl.ds(column, BLK)] for ref in (own, one, two, three)]
                here = jnp.where(hop == 0, here[0], jnp.where(hop == 1, here[1], jnp.where(hop == 2, here[2], here[3])))
                tiles.append(jnp.where(holder % 2 == core, here, there))
            pair = jnp.concatenate(tiles, axis=1)
            pair = pltpu.roll(pair, (4 - y) % 4 * 64, 1)
            for copy in range(8):
                out[copy, :, (side * 4 + k) * 256:(side * 4 + k + 1) * 256] = pair


def dot(first, second, axis):
    return lax.dot_general(
        first, second, (((axis,), (0,)), ((), ())), precision=HI, preferred_element_type=jnp.float32
    )


def vmem():
    return pl.BlockSpec(memory_space=pltpu.VMEM)


def smem():
    return pl.BlockSpec(memory_space=pltpu.SMEM)


def anywhere():
    return pl.BlockSpec(memory_space=pl.ANY)


def shift(block, axis, k):
    return lax.ppermute(block, axis, [(i, (i + k) % 4) for i in range(4)])


def turn(block, k):
    pairs = []
    for a in range(8):
        for b in range(4):
            for c in range(8):
                target = (a // 2 - k) % 4 * 2 + a % 2
                pairs.append(((a * 4 + b) * 8 + c, (c * 4 + b) * 8 + target))
    return lax.ppermute(block, AXES, pairs)


def at(array, index, axis=0):
    return lax.dynamic_index_in_dim(array, index, axis, keepdims=False)


def call(kernel, shapes, structure, *operands):
    return pl.pallas_call(
        kernel,
        out_shape=shapes,
        in_specs=[smem()] + [vmem()] * len(operands),
        out_specs=jax.tree.map(lambda _: vmem(), shapes),
    )(structure, *operands)


def of(*shape):
    return jax.ShapeDtypeStruct(shape, jnp.float32)


def per_device(root_cov, structure, child_factor, child_diag):
    x, zl = lax.axis_index("x"), lax.axis_index("zl")
    zh, core = lax.axis_index("zh"), lax.axis_index("core")
    fours = lax.iota(jnp.int32, 4)

    sends = call(class_kernel, of(4, 64, 768), structure, root_cov)
    turned = [turn(child_factor, k) for k in range(4)]
    pieces = lax.all_to_all(sends.reshape(32, 8, 768), CLASSED, 0, 0)
    pieces, turned, factor = lax.optimization_barrier((pieces, turned, child_factor))

    cut = call(cut_kernel, [of(2, 8, 768)] * 4, structure, pieces)
    landed = [cut[0]] + [shift(cut[k], "zh", k) for k in (1, 2, 3)]
    give = jnp.stack([at(part, 1 - core) for part in landed])
    got = lax.ppermute(give, "core", SWAP)
    copies = call(columns_kernel, of(8, 8, 2048), structure, *landed, got)
    other = lax.ppermute(factor, "zl", SWAP)

    rows = lax.all_to_all(copies, GROUP, 0, 0).reshape(64, 2048)

    turned = jnp.stack(turned)
    near = [turned] + [shift(turned, "y", -k) for k in (1, 2, 3)]
    far = [lax.ppermute(part, "core", SWAP) for part in near]
    near = jnp.stack(near, axis=1).reshape(1024, 512)
    far = jnp.stack(far, axis=1).reshape(1024, 512)

    cross = -(dot(rows[:, :1024], near, 1) + dot(rows[:, 1024:], far, 1))
    cross, factor, other = lax.optimization_barrier((cross, factor, other))

    near = jnp.stack([cross] + [shift(cross, "zh", -k) for k in (1, 2, 3)])
    far = lax.ppermute(near, "core", SWAP)
    pair = jnp.stack([jnp.where(zl == core, factor, other), jnp.where(zl == core, other, factor)])
    pairs = jnp.stack([pair] + [shift(pair, "x", -k) for k in (1, 2, 3)])
    pairs = jnp.take(pairs, (zh - x + fours) % 4, axis=0)
    share = dot(near.reshape(256, 512), pairs[:, 0].reshape(256, 512), 0)
    share = share + dot(far.reshape(256, 512), pairs[:, 1].reshape(256, 512), 0)
    share, cross = lax.optimization_barrier((share, cross))
    y = lax.axis_index("y")
    slabs = share.reshape(4, 128, 512)
    got = [at(slabs, y)] + [shift(at(slabs, (y + k) % 4), "y", k) for k in (1, 2, 3)]
    child = child_diag - (got[0] + got[1] + got[2] + got[3])
    return turn(cross, 0), child


def solution(mesh):
    fine = Mesh(mesh.devices.reshape(SIZES), AXES)
    spec = P(ROWS, COLS)
    return jax.shard_map(
        per_device,
        mesh=fine,
        in_specs=(spec, P(), spec, spec),
        out_specs=(spec, spec),
        check_vma=False,
    )
```
